32 devices in a mesh: layer: 8 (over y, x, core), spec: 4 (over z).
Axes of the slice: x: 2, y: 2, z: 4, core: 2. Of those that a mesh axis runs over, the one named last changes fastest.
Arguments:
- start_lead: float32 [64], P('spec'), may hold values from 128 to 512
- start_field: float32 [64, 8, 16, 1024], P('spec', 'layer'), may hold values from -6 to 6
- diag_dual: float32 [64, 8, 16, 1024], P('spec', 'layer'), may hold values from 0.25 to 2
- coupling_dual: float32 [64, 8, 16, 1024], P('spec', 'layer'), may hold values from -5 to 5
- linear_table: float32 [10, 8, 16, 1024], P(None, 'layer'), may hold values from -0.03125 to 0.03125
- labels: int32 [64], P('spec'), may hold values from 0 to 9
- bias_dual: float32 [64], P('spec'), may hold values from -1 to 1
- kernels: float32 [8, 3, 3, 64, 64], P('layer'), may hold values from -0.25 to 0.25
Outputs:
- grad_diag: float32 [64, 8, 16, 1024], P('spec', 'layer')
- grad_coupling: float32 [64, 8, 16, 1024], P('spec', 'layer')
- grad_linear: float32 [64, 8, 16, 1024], P('spec', 'layer')
- grad_bias: float32 [64], P('spec')
- soft_max: float32 [64], P('spec')
The draws below stay inside these ranges and needn't reach their ends.
All inputs are finite; a program needn't handle non-finite values.
Results may differ from the reference program's by a relative error of at most 0.0003.
Values sent between devices are 32-bit elements; how exact they have to be, the bound alone decides.
A program may use at most 128 MiB of HBM per device.

```python
import math
import jax
import jax.numpy as jnp
from jax import lax

CH = 64
SIDE = 16
CLASSES = 10
ITERS = 4
SPEC_DEV = 16
LAYERS = 8
SPECS = 64
N_SPEC = 4


def touch_ends(entries, key, smallest, largest):
    spot = [jax.random.randint(jax.random.fold_in(key, axis), (), 0, length) for axis, length in enumerate(entries.shape)]
    main_axis = entries.shape.index(max(entries.shape))
    beside = spot[:main_axis] + [(spot[main_axis] + 1) % entries.shape[main_axis]] + spot[main_axis + 1:]
    return entries.at[tuple(spot)].set(smallest).at[tuple(beside)].set(largest)


def block_levels(own_key, extent, pieces, low, largest):
    loudness = 1.0
    for dim, blocks in pieces:
        heights = jax.random.uniform(jax.random.fold_in(jax.random.fold_in(own_key, 6), dim), (blocks,), jnp.float32, low / len(pieces), largest / len(pieces))
        loudness = loudness * jnp.repeat(jnp.exp(heights), extent[dim] // blocks).reshape((-1,) + (1,) * (len(extent) - 1 - dim))
    return loudness


def scatter_about(own_key, extent, width, most, pieces=(), held_as=jnp.bfloat16):
    array = jax.random.normal(own_key, extent, jnp.float32) * width
    if len(pieces) > 0:
        array = block_levels(own_key, extent, pieces, -0.22, 0.18) * array
    return jnp.clip(array, min=-most, max=most).astype(held_as)


def setup_inputs(seed: int = 0) -> dict:
    key_list = jax.random.split(jax.random.key(seed), 9)
    start_lead = jnp.clip(128.0 + 384.0 * jax.random.uniform(key_list[0], (SPECS,), jnp.float32) ** block_levels(key_list[0], (SPECS,), ((0, 4),), -0.2, 0.2), 128.0, 512.0)
    start_field = scatter_about(key_list[1], (SPECS, LAYERS, SIDE, SIDE * CH), 1.0, 6.0, ((0, 4), (1, 8)), jnp.float32)
    diag_dual = jnp.clip(0.25 + 1.75 * jax.random.uniform(key_list[2], (SPECS, LAYERS, SIDE, SIDE * CH), jnp.float32) ** block_levels(key_list[2], (SPECS, LAYERS, SIDE, SIDE * CH), ((0, 4), (1, 8)), -0.2, 0.2), 0.25, 2.0)
    coupling_dual = scatter_about(key_list[3], (SPECS, LAYERS, SIDE, SIDE * CH), 1.0, 5.0, ((0, 4), (1, 8)), jnp.float32)
    linear_table = scatter_about(key_list[4], (CLASSES, LAYERS, SIDE, SIDE * CH), (LAYERS * SIDE * SIDE * CH // 4) ** -0.5, 0.03125, ((1, 8),), jnp.float32)
    labels = touch_ends(jax.random.randint(key_list[5], (SPECS,), 0, CLASSES), jax.random.fold_in(key_list[5], 1), 0, CLASSES - 1).astype(jnp.int32)
    bias_dual = jnp.clip(jax.random.uniform(key_list[6], (SPECS,), jnp.float32, -1.0, 1.0) * block_levels(key_list[6], (SPECS,), ((0, 4),), -0.4, 0.0), -1.0, 1.0)
    kernels = scatter_about(key_list[7], (LAYERS, 3, 3, CH, CH), (9 * CH) ** -0.5, 0.25, ((0, 8),), jnp.float32)
    return {"start_lead": start_lead, "start_field": start_field, "diag_dual": diag_dual, "coupling_dual": coupling_dual, "linear_table": linear_table, "labels": labels, "bias_dual": bias_dual, "kernels": kernels}


highest = lax.Precision.HIGHEST

def pair_blocks(kernel):
    zero_tap = jnp.zeros_like(kernel[:, 0, 0])
    per_tap = []
    for tap_row in range(3):
        side_parts = []
        for tap_side in range(3):
            row_parts = []
            for in_pos in range(2):
                col_parts = []
                for out_pos in range(2):
                    tap_col = 2 * (tap_side - 1) + in_pos - out_pos + 1
                    col_parts.append(kernel[:, tap_row, tap_col] if 0 <= tap_col <= 2 else zero_tap)
                row_parts.append(jnp.concatenate(col_parts, axis=2))
            side_parts.append(jnp.concatenate(row_parts, axis=1))
        per_tap.append(jnp.concatenate(side_parts, axis=1))
    return jnp.stack(per_tap, axis=1)

def transposed(kernel):
    return jnp.swapaxes(kernel[:, ::-1, ::-1], 3, 4)

def summed(values):
    return lax.optimization_barrier(jnp.sum(values, axis=(1, 2, 3)))

def spread(values):
    return values[:, None, None, None]

def conv_pairs(values, blocks):
    num_batch, num_layers, num_rows, num_width = values.shape
    pair_width = blocks.shape[-1]
    num_groups = num_width // pair_width
    grouped = values.reshape(num_batch, num_layers, num_rows, num_groups, pair_width)
    padded = jnp.pad(grouped, ((0, 0), (0, 0), (1, 1), (1, 1), (0, 0)))
    stacked = jnp.concatenate([padded[:, :, :, 0:num_groups], padded[:, :, :, 1:num_groups + 1], padded[:, :, :, 2:num_groups + 2]], axis=4)
    result = jnp.zeros(grouped.shape, jnp.float32)
    for tap_row in range(3):
        result = result + jnp.einsum('blhgi,lio->blhgo', stacked[:, :, tap_row:tap_row + num_rows], blocks[:, tap_row], precision=highest)
    return result.reshape(values.shape)

def local_neighbours(images, scaled):
    empty = jnp.zeros_like(images[:, :1])
    prior_img = jnp.concatenate([empty, images[:, :-1]], axis=1)
    later_in = jnp.concatenate([scaled[:, 1:], empty], axis=1)
    return (prior_img, later_in)

def apply_dual(lead_now, field_now, diag_part, coupling, linear, blocks_fwd, blocks_back, neighbours):
    images = conv_pairs(field_now, blocks_fwd)
    scaled = coupling * field_now
    prior_img, later_in = neighbours(images, scaled)
    back_img = conv_pairs(later_in, blocks_back)
    image_field = diag_part * field_now - 0.5 * coupling * prior_img - 0.5 * back_img + 0.5 * linear * spread(lead_now)
    return (image_field, prior_img)

def finish(alphas, betas, basis_lead, basis_field, basis_image, unit_count):
    alpha_mat = jnp.stack(alphas, axis=1)
    beta_mat = jnp.concatenate([jnp.stack(betas, axis=1), jnp.zeros_like(alpha_mat[:, :1])], axis=1)
    count = alpha_mat.shape[1]
    identity = jnp.eye(count, dtype=jnp.float32)
    tri_mat = alpha_mat[:, :, None] * identity + beta_mat[:, :, None] * jnp.eye(count, k=1, dtype=jnp.float32) + beta_mat[:, None, :] * jnp.eye(count, k=-1, dtype=jnp.float32)
    sigma_all = jnp.sqrt(lax.optimization_barrier(jnp.sum(tri_mat * tri_mat, axis=(1, 2))))
    scaled_tri = tri_mat / (2.0 * sigma_all[:, None, None])
    expo_mat = jnp.broadcast_to(identity, tri_mat.shape)
    for degree in range(12, 0, -1):
        expo_mat = identity + jnp.einsum('bij,bjk->bik', scaled_tri, expo_mat, precision=highest) / degree
    for squaring in range(4):
        expo_mat = jnp.einsum('bij,bjk->bik', expo_mat, expo_mat, precision=highest)
    trace_val = jnp.trace(expo_mat, axis1=1, axis2=2)
    weights = expo_mat / trace_val[:, None, None]
    soft_max = lax.optimization_barrier(jnp.sum(weights * tri_mat, axis=(1, 2)))
    lead_stack = jnp.stack(basis_lead, axis=0)
    field_stack = jnp.stack(basis_field, axis=0)
    image_stack = jnp.stack(basis_image, axis=0)
    mixed_field = jnp.einsum('bij,jblhw->iblhw', weights, field_stack, precision=highest)
    mixed_image = jnp.einsum('bij,jblhw->iblhw', weights, image_stack, precision=highest)
    grad_diag = unit_count * lax.optimization_barrier(jnp.sum(field_stack * mixed_field, axis=0))
    grad_coupling = -unit_count * lax.optimization_barrier(jnp.sum(field_stack * mixed_image, axis=0))
    grad_linear = math.sqrt(unit_count) * lax.optimization_barrier(jnp.sum(lead_stack[:, :, None, None, None] * mixed_field, axis=0))
    lead_rows = lead_stack.T
    grad_bias = lax.optimization_barrier(jnp.sum(weights * lead_rows[:, :, None] * lead_rows[:, None, :], axis=(1, 2)))
    return (grad_diag, grad_coupling, grad_linear, grad_bias, soft_max)

def lanczos(start_lead, start_field, diag_part, coupling, linear, bias_part, blocks_fwd, blocks_back):
    norm_start = start_lead * start_lead + summed(start_field * start_field)
    factor = 1.0 / jnp.sqrt(norm_start)
    lead_now = start_lead * factor
    field_now = start_field * spread(factor)
    lead_old = jnp.zeros_like(lead_now)
    field_old = jnp.zeros_like(field_now)
    beta_old = jnp.zeros_like(lead_now)
    alphas, betas, basis_lead, basis_field, basis_image = ([], [], [], [], [])
    for iteration in range(ITERS):
        image_field, prior_img = apply_dual(lead_now, field_now, diag_part, coupling, linear, blocks_fwd, blocks_back, local_neighbours)
        link_value = summed(linear * field_now)
        image_lead = bias_part * lead_now + 0.5 * link_value
        alpha_now = lead_now * image_lead + summed(field_now * image_field)
        alphas.append(alpha_now)
        basis_lead.append(lead_now)
        basis_field.append(field_now)
        basis_image.append(prior_img)
        if iteration < ITERS - 1:
            rest_lead = image_lead - alpha_now * lead_now - beta_old * lead_old
            rest_field = image_field - spread(alpha_now) * field_now - spread(beta_old) * field_old
            beta_now = jnp.sqrt(rest_lead * rest_lead + summed(rest_field * rest_field) + 1e-06)
            betas.append(beta_now)
            lead_old, field_old = (lead_now, field_now)
            lead_now = rest_lead / beta_now
            field_now = rest_field / spread(beta_now)
            beta_old = beta_now
    unit_count = start_field.shape[1] * start_field.shape[2] * start_field.shape[3]
    return finish(alphas, betas, basis_lead, basis_field, basis_image, unit_count)

def reference(start_lead, start_field, diag_dual, coupling_dual, linear_table, labels, bias_dual, kernels):
    blocks_fwd = pair_blocks(kernels)
    blocks_back = pair_blocks(transposed(kernels))

    def one_group(items):
        lead_part, field_part, diag_part, coupling, label_part, bias_part = items
        onehot = (label_part[:, None] == jnp.arange(CLASSES, dtype=jnp.int32)[None, :]).astype(jnp.float32)
        linear = jnp.einsum('sc,clhw->slhw', onehot, linear_table, precision=highest)
        return lanczos(lead_part, field_part, diag_part, coupling, linear, bias_part, blocks_fwd, blocks_back)

    def grouped(values):
        return values.reshape((N_SPEC, SPEC_DEV) + values.shape[1:])
    results = lax.map(one_group, (grouped(start_lead), grouped(start_field), grouped(diag_dual), grouped(coupling_dual), grouped(labels), grouped(bias_dual)))
    grad_diag, grad_coupling, grad_linear, grad_bias, soft_max = results
    full_shape = start_field.shape
    return (grad_diag.reshape(full_shape), grad_coupling.reshape(full_shape), grad_linear.reshape(full_shape), grad_bias.reshape(-1), soft_max.reshape(-1))
```

```python
import functools
import math

import jax
import jax.numpy as jnp
from jax import lax
from jax.experimental import pallas as pl
from jax.experimental.pallas import tpu as pltpu
from jax.sharding import PartitionSpec as P

ITERS = 4
CHUNKS = 2
LANES = 128
MESH = pl.DeviceIdType.MESH


def pair_weights(kernel):
    zero = jnp.zeros_like(kernel[0, 0])
    rows = []
    for in_pos in range(4):
        cols = []
        for tap_row in range(3):
            for out_pos in range(2):
                tap = in_pos - out_pos
                cols.append(kernel[tap_row, tap] if 0 <= tap <= 2 else zero)
        rows.append(jnp.concatenate(cols, axis=1))
    return jnp.concatenate(rows, axis=0)


def kernel_body(
    sections,
    unit_count,
    labels,
    lead0,
    start,
    diag,
    coup,
    table,
    bias,
    wf32,
    wb32,
    grad_diag,
    grad_coup,
    grad_lin,
    small,
    z,
    img,
    rec,
    send_img,
    send_scl,
    w_buf,
    back,
    xh,
    xl,
    wfh,
    wfl,
    wbh,
    wbl,
    part,
    coef,
    lead_b,
    pk,
    gath,
    s_img_s,
    s_img_r,
    s_scl_s,
    s_scl_r,
    s_pk_s,
    s_pk_r,
):
    me = lax.axis_index("layer")
    specs, rows, width = start.shape
    per = specs // CHUNKS
    num_groups = width // LANES
    half = LANES // 2
    block_rows = per * rows

    barrier = pltpu.get_barrier_semaphore()
    for hop in range(1, sections):
        peer = lax.rem(me + hop, sections)
        pl.semaphore_signal(barrier, inc=1, device_id={"layer": peer}, device_id_type=MESH)

    for src, hi, lo in ((wf32, wfh, wfl), (wb32, wbh, wbl)):
        val = src[...]
        top = val.astype(jnp.bfloat16)
        hi[...] = top
        lo[...] = (val - top.astype(jnp.float32)).astype(jnp.bfloat16)

    def img_copy(j, c):
        sl = pl.ds(c * per, per)
        return pltpu.make_async_remote_copy(
            src_ref=send_img.at[j, sl],
            dst_ref=img.at[j, sl],
            send_sem=s_img_s.at[j, c],
            recv_sem=s_img_r.at[j, c],
            device_id={"layer": lax.rem(me + 1, sections)},
            device_id_type=MESH,
        )

    def scl_copy(j, c):
        sl = pl.ds(c * per, per)
        return pltpu.make_async_remote_copy(
            src_ref=send_scl.at[j, sl],
            dst_ref=rec.at[j, sl],
            send_sem=s_scl_s.at[j, c],
            recv_sem=s_scl_r.at[j, c],
            device_id={"layer": lax.rem(me + sections - 1, sections)},
            device_id_type=MESH,
        )

    def pk_copy(j, c, hop):
        par = j % 2
        return pltpu.make_async_remote_copy(
            src_ref=pk.at[par, c],
            dst_ref=gath.at[par, c, me],
            send_sem=s_pk_s.at[par, c, hop],
            recv_sem=s_pk_r.at[par, c, hop],
            device_id={"layer": lax.rem(me + hop, sections)},
            device_id_type=MESH,
        )

    def put_shifted(s, val):
        wide = jnp.concatenate([val, jnp.zeros((rows, LANES), jnp.float32)], axis=1)
        wide = pltpu.roll(wide, half, 1)
        top = wide.astype(jnp.bfloat16)
        at = pl.ds(pl.multiple_of(s * rows, rows), rows)
        xh[at, :] = top
        xl[at, :] = (wide - top.astype(jnp.float32)).astype(jnp.bfloat16)

    def conv(hi_w, lo_w, write):
        row = lax.rem(lax.broadcasted_iota(jnp.int32, (block_rows, LANES), 0), rows)

        def step(g, carry):
            cols = pl.ds(pl.multiple_of(g * LANES, LANES), 2 * LANES)
            a_hi = xh[:, cols]
            a_lo = xl[:, cols]
            w_hi = hi_w[...]
            prod = jnp.dot(a_hi, w_hi, preferred_element_type=jnp.float32)
            prod += jnp.dot(a_lo, w_hi, preferred_element_type=jnp.float32)
            prod += jnp.dot(a_hi, lo_w[...], preferred_element_type=jnp.float32)
            above = pltpu.roll(prod[:, :LANES], 1, 0)
            below = pltpu.roll(prod[:, 2 * LANES :], block_rows - 1, 0)
            out = prod[:, LANES : 2 * LANES]
            out += jnp.where(row == 0, 0.0, above)
            out += jnp.where(row == rows - 1, 0.0, below)
            write(g, out.reshape(per, rows, LANES))
            return carry

        lax.fori_loop(0, num_groups, step, 0)

    def wide_row(k, s):
        cf = coef[k, pl.ds(s, 1), :]
        return jnp.concatenate([cf] * num_groups, axis=1)

    def forward(j, c):
        if j < ITERS - 1:

            @pl.when(me > 0)
            def _():
                scl_copy(j, c).start()

        @pl.when(me < sections - 1)
        def _():
            def write(g, out):
                send_img[j, pl.ds(c * per, per), :, pl.ds(pl.multiple_of(g * LANES, LANES), LANES)] = out

            conv(wfh, wfl, write)
            img_copy(j, c).start()

    def fold(val):
        acc = val[:, :LANES]
        for g in range(1, num_groups):
            acc = acc + val[:, g * LANES : (g + 1) * LANES]
        return jnp.sum(acc, axis=0, keepdims=True)

    def apply(j, c):
        last = j == ITERS - 1

        @pl.when(me > 0)
        def _():
            img_copy(j, c).wait_recv()

        if not last:

            @pl.when(me < sections - 1)
            def _():
                scl_copy(j, c).wait_recv()

                def shift_one(s, carry):
                    put_shifted(s, rec[j, c * per + s])
                    return carry

                lax.fori_loop(0, per, shift_one, 0)

                def write(g, out):
                    back[:, :, pl.ds(pl.multiple_of(g * LANES, LANES), LANES)] = out

                conv(wbh, wbl, write)

        coef[0] = lead_b[j, c]

        def one(s, carry):
            sp = c * per + s
            zs = z[j, sp]
            lin = table[labels[sp]]
            if last:
                w = diag[sp] * zs - coup[sp] * img[j, sp]
            else:
                w = diag[sp] * zs - 0.5 * (coup[sp] * img[j, sp] + back[s])
            w = w + lin * (0.5 * wide_row(0, s))
            part[0, pl.ds(s, 1), :] = fold(lin * zs)
            part[1, pl.ds(s, 1), :] = fold(zs * w)
            if not last:
                w_buf[sp] = w
                part[2, pl.ds(s, 1), :] = fold(w * w)
            if j == 0:
                part[3, pl.ds(s, 1), :] = fold(zs * zs)
            return carry

        lax.fori_loop(0, per, one, 0)
        lane = lax.broadcasted_iota(jnp.int32, (per, LANES), 1)
        packet = jnp.zeros((per, LANES), jnp.float32)
        for k in range(4 if j == 0 else (2 if last else 3)):
            packet = jnp.where(lane == k, jnp.sum(part[k], axis=1, keepdims=True), packet)
        pk[j % 2, c] = packet
        gath[j % 2, c, me] = packet
        for hop in range(1, sections):
            pk_copy(j, c, hop).start()

    def totals(j, c, count):
        for hop in range(1, sections):
            pk_copy(j, c, hop).wait()
        total = gath[j % 2, c, 0]
        for peer in range(1, sections):
            total = total + gath[j % 2, c, peer]
        return [jnp.broadcast_to(total[:, k : k + 1], (per, LANES)) for k in range(count)]

    @pl.when(me == 0)
    def _():
        def clear(s, carry):
            for j in range(ITERS):
                img[j, s] = jnp.zeros((rows, width), jnp.float32)
            return carry

        lax.fori_loop(0, specs, clear, 0)

    @pl.when(me == sections - 1)
    def _():
        def clear(s, carry):
            back[s] = jnp.zeros((rows, width), jnp.float32)
            return carry

        lax.fori_loop(0, per, clear, 0)

    pl.semaphore_wait(barrier, sections - 1)

    state = [{"alpha": [], "beta": []} for _ in range(CHUNKS)]
    for c in range(CHUNKS):
        lead_b[0, c] = jnp.broadcast_to(lead0[c * per : (c + 1) * per, :], (per, LANES))

        def first(s, carry):
            sp = c * per + s
            val = start[sp]
            z[0, sp] = val
            send_scl[0, sp] = coup[sp] * val
            put_shifted(s, val)
            return carry

        lax.fori_loop(0, per, first, 0)
        forward(0, c)

    for j in range(ITERS - 1):
        for c in range(CHUNKS):
            apply(j, c)
            st = state[c]
            bias_c = jnp.broadcast_to(bias[c * per : (c + 1) * per, :], (per, LANES))
            sums = totals(j, c, 4 if j == 0 else 3)
            lead_now = lead_b[j, c]
            image_lead = bias_c * lead_now + 0.5 * sums[0]
            if j == 0:
                factor = 1.0 / jnp.sqrt(lead_now * lead_now + sums[3])
                st["factor"] = factor
                alpha = factor * factor * (lead_now * image_lead + sums[1])
                lead_now = lead_now * factor
                image_lead = image_lead * factor
                power = factor * factor * sums[2]
                rest_lead = image_lead - alpha * lead_now
                beta = jnp.sqrt(image_lead * image_lead + power - alpha * alpha + 1e-06)
                inv = factor / beta
                lead_b[0, c] = lead_now
                coef[1] = inv
                coef[2] = -alpha * inv
            else:
                beta_old = st["beta"][-1]
                lead_old = lead_b[j - 1, c]
                alpha = lead_now * image_lead + sums[1]
                rest_lead = image_lead - alpha * lead_now - beta_old * lead_old
                beta = jnp.sqrt(image_lead * image_lead + sums[2] - alpha * alpha - beta_old * beta_old + 1e-06)
                inv = 1.0 / beta
                coef[1] = inv
                coef[2] = -alpha * inv
                coef[3] = -beta_old * inv * (st["factor"] if j == 1 else 1.0)
            lead_b[j + 1, c] = rest_lead / beta
            st["alpha"].append(alpha)
            st["beta"].append(beta)

            def advance(s, carry):
                sp = c * per + s
                val = w_buf[sp] * wide_row(1, s) + z[j, sp] * wide_row(2, s)
                if j > 0:
                    val = val + z[j - 1, sp] * wide_row(3, s)
                z[j + 1, sp] = val
                if j + 1 < ITERS - 1:
                    send_scl[j + 1, sp] = coup[sp] * val
                put_shifted(s, val)
                return carry

            lax.fori_loop(0, per, advance, 0)
            forward(j + 1, c)

    lane = lax.broadcasted_iota(jnp.int32, (per, LANES), 1)
    last = ITERS - 1
    for c in range(CHUNKS):
        apply(last, c)
    for c in range(CHUNKS):
        st = state[c]
        bias_c = jnp.broadcast_to(bias[c * per : (c + 1) * per, :], (per, LANES))
        sums = totals(last, c, 2)
        lead_now = lead_b[last, c]
        alpha = lead_now * (bias_c * lead_now + 0.5 * sums[0]) + sums[1]
        alphas = st["alpha"] + [alpha]
        betas = st["beta"]
        n = ITERS
        zero = jnp.zeros((per, LANES), jnp.float32)
        tri = [[zero] * n for _ in range(n)]
        norm = zero
        for i in range(n):
            tri[i][i] = alphas[i]
            norm = norm + alphas[i] * alphas[i]
            if i + 1 < n:
                tri[i][i + 1] = betas[i]
                tri[i + 1][i] = betas[i]
                norm = norm + 2.0 * (betas[i] * betas[i])
        scale = 0.5 / jnp.sqrt(norm)
        sx = [[tri[i][k] * scale for k in range(n)] for i in range(n)]
        expo = [[zero + (1.0 if i == k else 0.0) for k in range(n)] for i in range(n)]
        for degree in range(12, 0, -1):
            nxt = []
            for i in range(n):
                line = []
                for k in range(n):
                    acc = None
                    for m in range(max(0, i - 1), min(n, i + 2)):
                        term = sx[i][m] * expo[m][k]
                        acc = term if acc is None else acc + term
                    acc = acc * (1.0 / degree)
                    line.append(acc + 1.0 if i == k else acc)
                nxt.append(line)
            expo = nxt
        for _ in range(4):
            nxt = [[None] * n for _ in range(n)]
            for i in range(n):
                for k in range(n):
                    acc = expo[i][0] * expo[0][k]
                    for m in range(1, n):
                        acc = acc + expo[i][m] * expo[m][k]
                    nxt[i][k] = acc
            expo = nxt
        trace = expo[0][0] + expo[1][1] + expo[2][2] + expo[3][3]
        inv = 1.0 / trace
        wt = [[expo[i][k] * inv for k in range(n)] for i in range(n)]
        soft = zero
        gbias = zero
        leads = [lead_b[i, c] for i in range(n)]
        for i in range(n):
            for k in range(n):
                if abs(i - k) <= 1:
                    soft = soft + wt[i][k] * tri[i][k]
                gbias = gbias + wt[i][k] * (leads[i] * leads[k])
        small[c * per : (c + 1) * per, :] = jnp.where(lane == 0, gbias, soft)
        fac = [st["factor"], None, None, None]

        def scaled_by(val, *which):
            for i in which:
                if fac[i] is not None:
                    val = val * fac[i]
            return val

        slot = 0
        pair_slot = {}
        for i in range(n):
            for k in range(i, n):
                val = wt[i][k] if i == k else wt[i][k] + wt[k][i]
                coef[slot] = unit_count * scaled_by(val, i, k)
                pair_slot[i, k] = slot
                slot += 1
        mix_slot = {}
        for i in range(n):
            for k in range(n):
                coef[slot] = -unit_count * scaled_by(wt[i][k], i, k)
                mix_slot[i, k] = slot
                slot += 1
        lin_slot = {}
        for k in range(n):
            val = wt[0][k] * leads[0]
            for i in range(1, n):
                val = val + wt[i][k] * leads[i]
            coef[slot] = math.sqrt(unit_count) * scaled_by(val, k)
            lin_slot[k] = slot
            slot += 1

        def final(s, carry):
            sp = c * per + s
            cf = [coef[k, pl.ds(s, 1), :] for k in range(slot)]
            for g in range(num_groups):
                cols = slice(g * LANES, (g + 1) * LANES)
                zs = [z[i, sp, :, cols] for i in range(n)]
                ims = [img[i, sp, :, cols] for i in range(n)]
                gd = gc = gl = None
                for i in range(n):
                    mixed = zs[i] * cf[pair_slot[i, i]]
                    for k in range(i + 1, n):
                        mixed = mixed + zs[k] * cf[pair_slot[i, k]]
                    mixed_img = ims[0] * cf[mix_slot[i, 0]]
                    for k in range(1, n):
                        mixed_img = mixed_img + ims[k] * cf[mix_slot[i, k]]
                    gd = zs[i] * mixed if gd is None else gd + zs[i] * mixed
                    gc = zs[i] * mixed_img if gc is None else gc + zs[i] * mixed_img
                    lin = zs[i] * cf[lin_slot[i]]
                    gl = lin if gl is None else gl + lin
                grad_diag[sp, :, cols] = gd
                grad_coup[sp, :, cols] = gc
                grad_lin[sp, :, cols] = gl
            return carry

        lax.fori_loop(0, per, final, 0)

    @pl.when(me < sections - 1)
    def _():
        for j in range(ITERS):
            for c in range(CHUNKS):
                img_copy(j, c).wait_send()

    @pl.when(me > 0)
    def _():
        for j in range(ITERS - 1):
            for c in range(CHUNKS):
                scl_copy(j, c).wait_send()


def body(start_lead, start_field, diag_dual, coupling_dual, linear_table, labels, bias_dual, kernels):
    sections = lax.axis_size("layer")
    specs, _, rows, width = start_field.shape
    unit_count = sections * rows * width
    per = specs // CHUNKS
    kern = kernels[0]
    wf = pair_weights(kern)
    wb = pair_weights(jnp.swapaxes(kern[::-1, ::-1], 2, 3))
    shape3 = (specs, rows, width)
    full = pl.BlockSpec(memory_space=pltpu.VMEM)
    f32, bf16 = jnp.float32, jnp.bfloat16
    dma = pltpu.SemaphoreType.DMA
    outs = pl.pallas_call(
        functools.partial(kernel_body, sections, float(unit_count)),
        out_shape=[jax.ShapeDtypeStruct(shape3, f32)] * 3 + [jax.ShapeDtypeStruct((specs, LANES), f32)],
        in_specs=[pl.BlockSpec(memory_space=pltpu.SMEM)] + [full] * 8,
        out_specs=[full] * 4,
        scratch_shapes=[
            pltpu.VMEM((ITERS,) + shape3, f32),
            pltpu.VMEM((ITERS,) + shape3, f32),
            pltpu.VMEM((ITERS - 1,) + shape3, f32),
            pltpu.VMEM((ITERS,) + shape3, f32),
            pltpu.VMEM((ITERS - 1,) + shape3, f32),
            pltpu.VMEM(shape3, f32),
            pltpu.VMEM((per, rows, width), f32),
            pltpu.VMEM((per * rows, width + LANES), bf16),
            pltpu.VMEM((per * rows, width + LANES), bf16),
            pltpu.VMEM(wf.shape, bf16),
            pltpu.VMEM(wf.shape, bf16),
            pltpu.VMEM(wf.shape, bf16),
            pltpu.VMEM(wf.shape, bf16),
            pltpu.VMEM((4, per, LANES), f32),
            pltpu.VMEM((32, per, LANES), f32),
            pltpu.VMEM((ITERS, CHUNKS, per, LANES), f32),
            pltpu.VMEM((2, CHUNKS, per, LANES), f32),
            pltpu.VMEM((2, CHUNKS, sections, per, LANES), f32),
            dma((ITERS, CHUNKS)),
            dma((ITERS, CHUNKS)),
            dma((ITERS - 1, CHUNKS)),
            dma((ITERS - 1, CHUNKS)),
            dma((2, CHUNKS, sections)),
            dma((2, CHUNKS, sections)),
        ],
        compiler_params=pltpu.CompilerParams(collective_id=0, has_side_effects=True, vmem_limit_bytes=56 * 1024 * 1024),
    )(
        labels,
        start_lead[:, None],
        start_field.reshape(shape3),
        diag_dual.reshape(shape3),
        coupling_dual.reshape(shape3),
        linear_table.reshape(linear_table.shape[0], rows, width),
        bias_dual[:, None],
        wf,
        wb,
    )
    big = [out.reshape(start_field.shape) for out in outs[:3]]
    return (*big, outs[3][:, 0], outs[3][:, 1])


def solution(mesh):
    placed = (
        P("spec"),
        P("spec", "layer", None, None),
        P("spec", "layer", None, None),
        P("spec", "layer", None, None),
        P(None, "layer", None, None),
        P("spec"),
        P("spec"),
        P("layer", None, None, None, None),
    )
    return jax.shard_map(
        body,
        mesh=mesh,
        in_specs=placed,
        out_specs=(
            P("spec", "layer", None, None),
            P("spec", "layer", None, None),
            P("spec", "layer", None, None),
            P("spec"),
            P("spec"),
        ),
        check_vma=False,
    )
```

```python
import functools
import math

import jax
import jax.numpy as jnp
from jax import lax
from jax.experimental import pallas as pl
from jax.experimental.pallas import tpu as pltpu
from jax.sharding import PartitionSpec as P

ITERS = 4
CHUNKS = 2
LANES = 128
MESH = pl.DeviceIdType.MESH


def kernel_body(
    sections,
    unit_count,
    labels,
    lead0,
    start,
    diag,
    coup,
    table,
    bias,
    kern,
    grad_diag,
    grad_coup,
    grad_lin,
    small,
    z,
    img,
    rec,
    send_img,
    send_scl,
    w_buf,
    back,
    xh,
    xl,
    wfh,
    wfl,
    wbh,
    wbl,
    part,
    coef,
    lead_b,
    pk,
    gath,
    s_img_s,
    s_img_r,
    s_scl_s,
    s_scl_r,
    s_pk_s,
    s_pk_r,
):
    me = lax.axis_index("layer")
    specs, rows, width = start.shape
    per = specs // CHUNKS
    num_groups = width // LANES
    half = LANES // 2
    block_rows = per * rows

    barrier = pltpu.get_barrier_semaphore()
    for hop in range(1, sections):
        peer = lax.rem(me + hop, sections)
        pl.semaphore_signal(barrier, inc=1, device_id={"layer": peer}, device_id_type=MESH)

    chan = kern.shape[-1]
    zero_tap = jnp.zeros((chan, chan), jnp.float32)
    for tap_row in range(3):
        fwd_taps = [kern[tap_row, tap] for tap in range(3)]
        back_taps = [jnp.transpose(kern[2 - tap_row, 2 - tap]) for tap in range(3)]
        for taps, hi, lo in ((fwd_taps, wfh, wfl), (back_taps, wbh, wbl)):
            for in_pos in range(4):
                pieces = [taps[in_pos - q] if 0 <= in_pos - q <= 2 else zero_tap for q in range(2)]
                val = jnp.concatenate(pieces, axis=1)
                top = val.astype(jnp.bfloat16)
                at = (slice(in_pos * chan, (in_pos + 1) * chan), slice(tap_row * LANES, (tap_row + 1) * LANES))
                hi[at] = top
                lo[at] = (val - top.astype(jnp.float32)).astype(jnp.bfloat16)

    def img_copy(j, c):
        sl = pl.ds(c * per, per)
        return pltpu.make_async_remote_copy(
            src_ref=send_img.at[j, sl],
            dst_ref=img.at[j, sl],
            send_sem=s_img_s.at[j, c],
            recv_sem=s_img_r.at[j, c],
            device_id={"layer": lax.rem(me + 1, sections)},
            device_id_type=MESH,
        )

    def scl_copy(j, c):
        sl = pl.ds(c * per, per)
        return pltpu.make_async_remote_copy(
            src_ref=send_scl.at[j, sl],
            dst_ref=rec.at[j, sl],
            send_sem=s_scl_s.at[j, c],
            recv_sem=s_scl_r.at[j, c],
            device_id={"layer": lax.rem(me + sections - 1, sections)},
            device_id_type=MESH,
        )

    def pk_copy(j, c, hop):
        par = j % 2
        return pltpu.make_async_remote_copy(
            src_ref=pk.at[par, c],
            dst_ref=gath.at[par, c, me],
            send_sem=s_pk_s.at[par, c, hop],
            recv_sem=s_pk_r.at[par, c, hop],
            device_id={"layer": lax.rem(me + hop, sections)},
            device_id_type=MESH,
        )

    def put_shifted(s, val):
        wide = jnp.concatenate([val, jnp.zeros((rows, LANES), jnp.float32)], axis=1)
        wide = pltpu.roll(wide, half, 1)
        top = wide.astype(jnp.bfloat16)
        at = pl.ds(pl.multiple_of(s * rows, rows), rows)
        xh[at, :] = top
        xl[at, :] = (wide - top.astype(jnp.float32)).astype(jnp.bfloat16)

    def conv(hi_w, lo_w, write):
        row = lax.rem(lax.broadcasted_iota(jnp.int32, (block_rows, LANES), 0), rows)

        def step(g, carry):
            cols = pl.ds(pl.multiple_of(g * LANES, LANES), 2 * LANES)
            a_hi = xh[:, cols]
            a_lo = xl[:, cols]
            w_hi = hi_w[...]
            prod = jnp.dot(a_hi, w_hi, preferred_element_type=jnp.float32)
            prod += jnp.dot(a_lo, w_hi, preferred_element_type=jnp.float32)
            prod += jnp.dot(a_hi, lo_w[...], preferred_element_type=jnp.float32)
            above = pltpu.roll(prod[:, :LANES], 1, 0)
            below = pltpu.roll(prod[:, 2 * LANES :], block_rows - 1, 0)
            out = prod[:, LANES : 2 * LANES]
            out += jnp.where(row == 0, 0.0, above)
            out += jnp.where(row == rows - 1, 0.0, below)
            write(g, out.reshape(per, rows, LANES))
            return carry

        lax.fori_loop(0, num_groups, step, 0)

    def wide_row(k, s):
        cf = coef[k, pl.ds(s, 1), :]
        return jnp.concatenate([cf] * num_groups, axis=1)

    def forward(j, c):
        if j < ITERS - 1:

            @pl.when(me > 0)
            def _():
                scl_copy(j, c).start()

        @pl.when(me < sections - 1)
        def _():
            def write(g, out):
                send_img[j, pl.ds(c * per, per), :, pl.ds(pl.multiple_of(g * LANES, LANES), LANES)] = out

            conv(wfh, wfl, write)
            img_copy(j, c).start()

    def fold(val):
        acc = val[:, :LANES]
        for g in range(1, num_groups):
            acc = acc + val[:, g * LANES : (g + 1) * LANES]
        return jnp.sum(acc, axis=0, keepdims=True)

    def recur(ref, val, j, sp, s):
        val = val * wide_row(1, s) + ref[j - 1, sp] * wide_row(2, s)
        if j > 1:
            val = val + ref[j - 2, sp] * wide_row(3, s)
        return val

    def apply(j, c):
        last = j == ITERS - 1

        @pl.when(me > 0)
        def _():
            img_copy(j, c).wait_recv()

        if not last:

            @pl.when(me < sections - 1)
            def _():
                scl_copy(j, c).wait_recv()

                def shift_one(s, carry):
                    val = rec[j, c * per + s]
                    if j > 0:
                        val = recur(rec, val, j, c * per + s, s)
                        rec[j, c * per + s] = val
                    put_shifted(s, val)
                    return carry

                lax.fori_loop(0, per, shift_one, 0)

                def write(g, out):
                    back[:, :, pl.ds(pl.multiple_of(g * LANES, LANES), LANES)] = out

                conv(wbh, wbl, write)

        coef[0] = lead_b[j, c]

        def one(s, carry):
            sp = c * per + s
            zs = z[j, sp]
            lin = table[labels[sp]]
            image = img[j, sp]
            if j > 0:
                image = recur(img, image, j, sp, s)
                img[j, sp] = image
            if last:
                w = diag[sp] * zs - coup[sp] * image
            else:
                w = diag[sp] * zs - 0.5 * (coup[sp] * image + back[s])
            w = w + lin * (0.5 * wide_row(0, s))
            part[0, pl.ds(s, 1), :] = fold(lin * zs)
            part[1, pl.ds(s, 1), :] = fold(zs * w)
            if not last:
                w_buf[sp] = w
                put_shifted(s, w)
                if j + 1 < ITERS - 1:
                    send_scl[j + 1, sp] = coup[sp] * w
                part[2, pl.ds(s, 1), :] = fold(w * w)
            if j == 0:
                part[3, pl.ds(s, 1), :] = fold(zs * zs)
            return carry

        lax.fori_loop(0, per, one, 0)
        lane = lax.broadcasted_iota(jnp.int32, (per, LANES), 1)
        packet = jnp.zeros((per, LANES), jnp.float32)
        for k in range(4 if j == 0 else (2 if last else 3)):
            packet = jnp.where(lane == k, jnp.sum(part[k], axis=1, keepdims=True), packet)
        pk[j % 2, c] = packet
        gath[j % 2, c, me] = packet
        for hop in range(1, sections):
            pk_copy(j, c, hop).start()

    def totals(j, c, count):
        for hop in range(1, sections):
            pk_copy(j, c, hop).wait()
        total = gath[j % 2, c, 0]
        for peer in range(1, sections):
            total = total + gath[j % 2, c, peer]
        return [jnp.broadcast_to(total[:, k : k + 1], (per, LANES)) for k in range(count)]

    @pl.when(me == 0)
    def _():
        def clear(s, carry):
            for j in range(ITERS):
                img[j, s] = jnp.zeros((rows, width), jnp.float32)
            return carry

        lax.fori_loop(0, specs, clear, 0)

    @pl.when(me == sections - 1)
    def _():
        def clear(s, carry):
            back[s] = jnp.zeros((rows, width), jnp.float32)
            return carry

        lax.fori_loop(0, per, clear, 0)

    pl.semaphore_wait(barrier, sections - 1)

    state = [{"alpha": [], "beta": []} for _ in range(CHUNKS)]
    for c in range(CHUNKS):
        lead_b[0, c] = jnp.broadcast_to(lead0[c * per : (c + 1) * per, :], (per, LANES))

        def first(s, carry):
            sp = c * per + s
            val = start[sp]
            z[0, sp] = val
            send_scl[0, sp] = coup[sp] * val
            put_shifted(s, val)
            return carry

        lax.fori_loop(0, per, first, 0)
        forward(0, c)

    for c in range(CHUNKS):
        apply(0, c)
        forward(1, c)
    for j in range(ITERS - 1):
        for c in range(CHUNKS):
            st = state[c]
            bias_c = jnp.broadcast_to(bias[c * per : (c + 1) * per, :], (per, LANES))
            sums = totals(j, c, 4 if j == 0 else 3)
            lead_now = lead_b[j, c]
            image_lead = bias_c * lead_now + 0.5 * sums[0]
            if j == 0:
                factor = 1.0 / jnp.sqrt(lead_now * lead_now + sums[3])
                st["factor"] = factor
                alpha = factor * factor * (lead_now * image_lead + sums[1])
                lead_now = lead_now * factor
                image_lead = image_lead * factor
                power = factor * factor * sums[2]
                rest_lead = image_lead - alpha * lead_now
                beta = jnp.sqrt(image_lead * image_lead + power - alpha * alpha + 1e-06)
                inv = factor / beta
                lead_b[0, c] = lead_now
                coef[1] = inv
                coef[2] = -alpha * inv
            else:
                beta_old = st["beta"][-1]
                lead_old = lead_b[j - 1, c]
                alpha = lead_now * image_lead + sums[1]
                rest_lead = image_lead - alpha * lead_now - beta_old * lead_old
                beta = jnp.sqrt(image_lead * image_lead + sums[2] - alpha * alpha - beta_old * beta_old + 1e-06)
                inv = 1.0 / beta
                coef[1] = inv
                coef[2] = -alpha * inv
                coef[3] = -beta_old * inv * (st["factor"] if j == 1 else 1.0)
            lead_b[j + 1, c] = rest_lead / beta
            st["alpha"].append(alpha)
            st["beta"].append(beta)

            def advance(s, carry):
                sp = c * per + s
                val = w_buf[sp] * wide_row(1, s) + z[j, sp] * wide_row(2, s)
                if j > 0:
                    val = val + z[j - 1, sp] * wide_row(3, s)
                z[j + 1, sp] = val
                return carry

            lax.fori_loop(0, per, advance, 0)
            apply(j + 1, c)
            if j + 1 < ITERS - 1:
                forward(j + 2, c)

    lane = lax.broadcasted_iota(jnp.int32, (per, LANES), 1)
    last = ITERS - 1
    for c in range(CHUNKS):
        st = state[c]
        bias_c = jnp.broadcast_to(bias[c * per : (c + 1) * per, :], (per, LANES))
        sums = totals(last, c, 2)
        lead_now = lead_b[last, c]
        alpha = lead_now * (bias_c * lead_now + 0.5 * sums[0]) + sums[1]
        alphas = st["alpha"] + [alpha]
        betas = st["beta"]
        n = ITERS
        zero = jnp.zeros((per, LANES), jnp.float32)
        tri = [[zero] * n for _ in range(n)]
        norm = zero
        for i in range(n):
            tri[i][i] = alphas[i]
            norm = norm + alphas[i] * alphas[i]
            if i + 1 < n:
                tri[i][i + 1] = betas[i]
                tri[i + 1][i] = betas[i]
                norm = norm + 2.0 * (betas[i] * betas[i])
        scale = 0.5 / jnp.sqrt(norm)
        sx = [[tri[i][k] * scale for k in range(n)] for i in range(n)]
        expo = [[zero + (1.0 if i == k else 0.0) for k in range(n)] for i in range(n)]
        for degree in range(12, 0, -1):
            nxt = []
            for i in range(n):
                line = []
                for k in range(n):
                    acc = None
                    for m in range(max(0, i - 1), min(n, i + 2)):
                        term = sx[i][m] * expo[m][k]
                        acc = term if acc is None else acc + term
                    acc = acc * (1.0 / degree)
                    line.append(acc + 1.0 if i == k else acc)
                nxt.append(line)
            expo = nxt
        for _ in range(4):
            nxt = [[None] * n for _ in range(n)]
            for i in range(n):
                for k in range(n):
                    acc = expo[i][0] * expo[0][k]
                    for m in range(1, n):
                        acc = acc + expo[i][m] * expo[m][k]
                    nxt[i][k] = acc
            expo = nxt
        trace = expo[0][0] + expo[1][1] + expo[2][2] + expo[3][3]
        inv = 1.0 / trace
        wt = [[expo[i][k] * inv for k in range(n)] for i in range(n)]
        soft = zero
        gbias = zero
        leads = [lead_b[i, c] for i in range(n)]
        for i in range(n):
            for k in range(n):
                if abs(i - k) <= 1:
                    soft = soft + wt[i][k] * tri[i][k]
                gbias = gbias + wt[i][k] * (leads[i] * leads[k])
        small[c * per : (c + 1) * per, :] = jnp.where(lane == 0, gbias, soft)
        fac = [st["factor"], None, None, None]

        def scaled_by(val, *which):
            for i in which:
                if fac[i] is not None:
                    val = val * fac[i]
            return val

        slot = 0
        pair_slot = {}
        for i in range(n):
            for k in range(i, n):
                val = wt[i][k] if i == k else wt[i][k] + wt[k][i]
                coef[slot] = unit_count * scaled_by(val, i, k)
                pair_slot[i, k] = slot
                slot += 1
        mix_slot = {}
        for i in range(n):
            for k in range(n):
                coef[slot] = -unit_count * scaled_by(wt[i][k], i, k)
                mix_slot[i, k] = slot
                slot += 1
        lin_slot = {}
        for k in range(n):
            val = wt[0][k] * leads[0]
            for i in range(1, n):
                val = val + wt[i][k] * leads[i]
            coef[slot] = math.sqrt(unit_count) * scaled_by(val, k)
            lin_slot[k] = slot
            slot += 1

        def final(s, carry):
            sp = c * per + s
            cf = [coef[k, pl.ds(s, 1), :] for k in range(slot)]
            for g in range(num_groups):
                cols = slice(g * LANES, (g + 1) * LANES)
                zs = [z[i, sp, :, cols] for i in range(n)]
                ims = [img[i, sp, :, cols] for i in range(n)]
                gd = gc = gl = None
                for i in range(n):
                    mixed = zs[i] * cf[pair_slot[i, i]]
                    for k in range(i + 1, n):
                        mixed = mixed + zs[k] * cf[pair_slot[i, k]]
                    mixed_img = ims[0] * cf[mix_slot[i, 0]]
                    for k in range(1, n):
                        mixed_img = mixed_img + ims[k] * cf[mix_slot[i, k]]
                    gd = zs[i] * mixed if gd is None else gd + zs[i] * mixed
                    gc = zs[i] * mixed_img if gc is None else gc + zs[i] * mixed_img
                    lin = zs[i] * cf[lin_slot[i]]
                    gl = lin if gl is None else gl + lin
                grad_diag[sp, :, cols] = gd
                grad_coup[sp, :, cols] = gc
                grad_lin[sp, :, cols] = gl
            return carry

        lax.fori_loop(0, per, final, 0)

    @pl.when(me < sections - 1)
    def _():
        for j in range(ITERS):
            for c in range(CHUNKS):
                img_copy(j, c).wait_send()

    @pl.when(me > 0)
    def _():
        for j in range(ITERS - 1):
            for c in range(CHUNKS):
                scl_copy(j, c).wait_send()


def body(start_lead, start_field, diag_dual, coupling_dual, linear_table, labels, bias_dual, kernels):
    sections = lax.axis_size("layer")
    specs, _, rows, width = start_field.shape
    unit_count = sections * rows * width
    per = specs // CHUNKS
    chan = kernels.shape[-1]
    shape3 = (specs, rows, width)
    full = pl.BlockSpec(memory_space=pltpu.VMEM)
    f32, bf16 = jnp.float32, jnp.bfloat16
    dma = pltpu.SemaphoreType.DMA
    outs = pl.pallas_call(
        functools.partial(kernel_body, sections, float(unit_count)),
        out_shape=[jax.ShapeDtypeStruct(shape3, f32)] * 3 + [jax.ShapeDtypeStruct((specs, LANES), f32)],
        in_specs=[pl.BlockSpec(memory_space=pltpu.SMEM)] + [full] * 7,
        out_specs=[full] * 4,
        scratch_shapes=[
            pltpu.VMEM((ITERS,) + shape3, f32),
            pltpu.VMEM((ITERS,) + shape3, f32),
            pltpu.VMEM((ITERS - 1,) + shape3, f32),
            pltpu.VMEM((ITERS,) + shape3, f32),
            pltpu.VMEM((ITERS - 1,) + shape3, f32),
            pltpu.VMEM(shape3, f32),
            pltpu.VMEM((per, rows, width), f32),
            pltpu.VMEM((per * rows, width + LANES), bf16),
            pltpu.VMEM((per * rows, width + LANES), bf16),
            pltpu.VMEM((4 * chan, 6 * chan), bf16),
            pltpu.VMEM((4 * chan, 6 * chan), bf16),
            pltpu.VMEM((4 * chan, 6 * chan), bf16),
            pltpu.VMEM((4 * chan, 6 * chan), bf16),
            pltpu.VMEM((4, per, LANES), f32),
            pltpu.VMEM((32, per, LANES), f32),
            pltpu.VMEM((ITERS, CHUNKS, per, LANES), f32),
            pltpu.VMEM((2, CHUNKS, per, LANES), f32),
            pltpu.VMEM((2, CHUNKS, sections, per, LANES), f32),
            dma((ITERS, CHUNKS)),
            dma((ITERS, CHUNKS)),
            dma((ITERS - 1, CHUNKS)),
            dma((ITERS - 1, CHUNKS)),
            dma((2, CHUNKS, sections)),
            dma((2, CHUNKS, sections)),
        ],
        compiler_params=pltpu.CompilerParams(collective_id=0, has_side_effects=True, vmem_limit_bytes=56 * 1024 * 1024),
    )(
        labels,
        start_lead[:, None],
        start_field.reshape(shape3),
        diag_dual.reshape(shape3),
        coupling_dual.reshape(shape3),
        linear_table.reshape(linear_table.shape[0], rows, width),
        bias_dual[:, None],
        kernels.reshape(kernels.shape[1:]),
    )
    big = [out.reshape(start_field.shape) for out in outs[:3]]
    return (*big, outs[3][:, 0], outs[3][:, 1])


def solution(mesh):
    placed = (
        P("spec"),
        P("spec", "layer", None, None),
        P("spec", "layer", None, None),
        P("spec", "layer", None, None),
        P(None, "layer", None, None),
        P("spec"),
        P("spec"),
        P("layer", None, None, None, None),
    )
    return jax.shard_map(
        body,
        mesh=mesh,
        in_specs=placed,
        out_specs=(
            P("spec", "layer", None, None),
            P("spec", "layer", None, None),
            P("spec", "layer", None, None),
            P("spec"),
            P("spec"),
        ),
        check_vma=False,
    )
```

```python
import functools
import math

import jax
import jax.numpy as jnp
from jax import lax
from jax.experimental import pallas as pl
from jax.experimental.pallas import tpu as pltpu
from jax.sharding import PartitionSpec as P

ITERS = 4
CHUNKS = 2
LANES = 128
RELAY_SECTIONS = 8
IMAGES_VIA_LAST = True
MESH = pl.DeviceIdType.MESH


def kernel_body(
    sections,
    unit_count,
    labels,
    lead0,
    start,
    diag,
    coup,
    table,
    bias,
    kern,
    grad_diag,
    grad_coup,
    grad_lin,
    small,
    z,
    img,
    rec,
    send_img,
    send_scl,
    w_buf,
    back,
    xh,
    xl,
    wfh,
    wfl,
    wbh,
    wbl,
    part,
    coef,
    lead_b,
    pk,
    gath,
    s_img_s,
    s_img_r,
    s_scl_s,
    s_scl_r,
    s_pk_s,
    s_pk_r,
    rly,
    s_in_s,
    s_in_r,
    s_out_s,
    s_out_r,
):
    me = lax.axis_index("layer")
    specs, rows, width = start.shape
    per = specs // CHUNKS
    num_groups = width // LANES
    half = LANES // 2
    block_rows = per * rows

    barrier = pltpu.get_barrier_semaphore()
    for hop in range(1, sections):
        peer = lax.rem(me + hop, sections)
        pl.semaphore_signal(barrier, inc=1, device_id={"layer": peer}, device_id_type=MESH)

    chan = kern.shape[-1]
    zero_tap = jnp.zeros((chan, chan), jnp.float32)
    for tap_row in range(3):
        fwd_taps = [kern[tap_row, tap] for tap in range(3)]
        back_taps = [jnp.transpose(kern[2 - tap_row, 2 - tap]) for tap in range(3)]
        for taps, hi, lo in ((fwd_taps, wfh, wfl), (back_taps, wbh, wbl)):
            for in_pos in range(4):
                pieces = [taps[in_pos - q] if 0 <= in_pos - q <= 2 else zero_tap for q in range(2)]
                val = jnp.concatenate(pieces, axis=1)
                top = val.astype(jnp.bfloat16)
                at = (slice(in_pos * chan, (in_pos + 1) * chan), slice(tap_row * LANES, (tap_row + 1) * LANES))
                hi[at] = top
                lo[at] = (val - top.astype(jnp.float32)).astype(jnp.bfloat16)

    relayed = sections == RELAY_SECTIONS
    low, high = sections // 2 - 1, sections // 2
    img_via, scl_via = (sections - 1, 0) if IMAGES_VIA_LAST else (0, sections - 1)
    direct = per // 2
    near = jnp.logical_and

    def relay_in(j, c, images):
        src = send_img if images else send_scl
        return pltpu.make_async_remote_copy(
            src_ref=src.at[j, pl.ds(c * per + direct, per - direct)],
            dst_ref=rly.at[j, pl.ds(c * (per - direct), per - direct)],
            send_sem=s_in_s.at[j, c],
            recv_sem=s_in_r.at[j, c],
            device_id={"layer": jnp.int32(img_via if images else scl_via)},
            device_id_type=MESH,
        )

    def relay_out(j, c, images):
        dst = img if images else rec
        return pltpu.make_async_remote_copy(
            src_ref=rly.at[j, pl.ds(c * (per - direct), per - direct)],
            dst_ref=dst.at[j, pl.ds(c * per + direct, per - direct)],
            send_sem=s_out_s.at[j, c],
            recv_sem=s_out_r.at[j, c],
            device_id={"layer": jnp.int32(high if images else low)},
            device_id_type=MESH,
        )

    def pass_on(j, c):
        if not relayed:
            return
        for images, via in ((True, img_via), (False, scl_via)):
            if images or j < ITERS - 1:

                @pl.when(me == via)
                def _():
                    relay_in(j, c, images).wait_recv()
                    relay_out(j, c, images).start()

    def each_copy(j, c, images, side, act):
        copy = img_copy if images else scl_copy
        if images:
            has = me < sections - 1 if side == 0 else me > 0
            middle = low if side == 0 else high
        else:
            has = me > 0 if side == 0 else me < sections - 1
            middle = high if side == 0 else low
        if not relayed:

            @pl.when(has)
            def _():
                act(copy(j, c))

            return

        @pl.when(near(has, me != middle))
        def _():
            act(copy(j, c))

        @pl.when(me == middle)
        def _():
            act(copy(j, c, direct))
            act(relay_in(j, c, images) if side == 0 else relay_out(j, c, images))

    def img_copy(j, c, count=per):
        sl = pl.ds(c * per, count)
        return pltpu.make_async_remote_copy(
            src_ref=send_img.at[j, sl],
            dst_ref=img.at[j, sl],
            send_sem=s_img_s.at[j, c],
            recv_sem=s_img_r.at[j, c],
            device_id={"layer": lax.rem(me + 1, sections)},
            device_id_type=MESH,
        )

    def scl_copy(j, c, count=per):
        sl = pl.ds(c * per, count)
        return pltpu.make_async_remote_copy(
            src_ref=send_scl.at[j, sl],
            dst_ref=rec.at[j, sl],
            send_sem=s_scl_s.at[j, c],
            recv_sem=s_scl_r.at[j, c],
            device_id={"layer": lax.rem(me + sections - 1, sections)},
            device_id_type=MESH,
        )

    def pk_copy(j, c, hop):
        par = j % 2
        return pltpu.make_async_remote_copy(
            src_ref=pk.at[par, c],
            dst_ref=gath.at[par, c, me],
            send_sem=s_pk_s.at[par, c, hop],
            recv_sem=s_pk_r.at[par, c, hop],
            device_id={"layer": lax.rem(me + hop, sections)},
            device_id_type=MESH,
        )

    def put_shifted(s, val):
        wide = jnp.concatenate([val, jnp.zeros((rows, LANES), jnp.float32)], axis=1)
        wide = pltpu.roll(wide, half, 1)
        top = wide.astype(jnp.bfloat16)
        at = pl.ds(pl.multiple_of(s * rows, rows), rows)
        xh[at, :] = top
        xl[at, :] = (wide - top.astype(jnp.float32)).astype(jnp.bfloat16)

    def conv(hi_w, lo_w, write):
        row = lax.rem(lax.broadcasted_iota(jnp.int32, (block_rows, LANES), 0), rows)

        def step(g, carry):
            cols = pl.ds(pl.multiple_of(g * LANES, LANES), 2 * LANES)
            a_hi = xh[:, cols]
            a_lo = xl[:, cols]
            w_hi = hi_w[...]
            prod = jnp.dot(a_hi, w_hi, preferred_element_type=jnp.float32)
            prod += jnp.dot(a_lo, w_hi, preferred_element_type=jnp.float32)
            prod += jnp.dot(a_hi, lo_w[...], preferred_element_type=jnp.float32)
            above = pltpu.roll(prod[:, :LANES], 1, 0)
            below = pltpu.roll(prod[:, 2 * LANES :], block_rows - 1, 0)
            out = prod[:, LANES : 2 * LANES]
            out += jnp.where(row == 0, 0.0, above)
            out += jnp.where(row == rows - 1, 0.0, below)
            write(g, out.reshape(per, rows, LANES))
            return carry

        lax.fori_loop(0, num_groups, step, 0)

    def wide_row(k, s):
        cf = coef[k, pl.ds(s, 1), :]
        return jnp.concatenate([cf] * num_groups, axis=1)

    def forward(j, c):
        if j < ITERS - 1:
            each_copy(j, c, False, 0, lambda copy: copy.start())

        @pl.when(me < sections - 1)
        def _():
            def write(g, out):
                send_img[j, pl.ds(c * per, per), :, pl.ds(pl.multiple_of(g * LANES, LANES), LANES)] = out

            conv(wfh, wfl, write)

        each_copy(j, c, True, 0, lambda copy: copy.start())

    def fold(val):
        acc = val[:, :LANES]
        for g in range(1, num_groups):
            acc = acc + val[:, g * LANES : (g + 1) * LANES]
        return jnp.sum(acc, axis=0, keepdims=True)

    def recur(ref, val, j, sp, s):
        val = val * wide_row(1, s) + ref[j - 1, sp] * wide_row(2, s)
        if j > 1:
            val = val + ref[j - 2, sp] * wide_row(3, s)
        return val

    def apply(j, c):
        last = j == ITERS - 1
        pass_on(j, c)
        each_copy(j, c, True, 1, lambda copy: copy.wait_recv())
        if not last:
            each_copy(j, c, False, 1, lambda copy: copy.wait_recv())

            @pl.when(me < sections - 1)
            def _():
                def shift_one(s, carry):
                    val = rec[j, c * per + s]
                    if j > 0:
                        val = recur(rec, val, j, c * per + s, s)
                        rec[j, c * per + s] = val
                    put_shifted(s, val)
                    return carry

                lax.fori_loop(0, per, shift_one, 0)

                def write(g, out):
                    back[:, :, pl.ds(pl.multiple_of(g * LANES, LANES), LANES)] = out

                conv(wbh, wbl, write)

        coef[0] = lead_b[j, c]

        def one(s, carry):
            sp = c * per + s
            zs = z[j, sp]
            lin = table[labels[sp]]
            image = img[j, sp]
            if j > 0:
                image = recur(img, image, j, sp, s)
                img[j, sp] = image
            if last:
                w = diag[sp] * zs - coup[sp] * image
            else:
                w = diag[sp] * zs - 0.5 * (coup[sp] * image + back[s])
            w = w + lin * (0.5 * wide_row(0, s))
            part[0, pl.ds(s, 1), :] = fold(lin * zs)
            part[1, pl.ds(s, 1), :] = fold(zs * w)
            if not last:
                w_buf[sp] = w
                put_shifted(s, w)
                if j + 1 < ITERS - 1:
                    send_scl[j + 1, sp] = coup[sp] * w
                part[2, pl.ds(s, 1), :] = fold(w * w)
            if j == 0:
                part[3, pl.ds(s, 1), :] = fold(zs * zs)
            return carry

        lax.fori_loop(0, per, one, 0)
        lane = lax.broadcasted_iota(jnp.int32, (per, LANES), 1)
        packet = jnp.zeros((per, LANES), jnp.float32)
        for k in range(4 if j == 0 else (2 if last else 3)):
            packet = jnp.where(lane == k, jnp.sum(part[k], axis=1, keepdims=True), packet)
        pk[j % 2, c] = packet
        gath[j % 2, c, me] = packet
        for hop in range(1, sections):
            pk_copy(j, c, hop).start()

    def totals(j, c, count):
        for hop in range(1, sections):
            pk_copy(j, c, hop).wait()
        total = gath[j % 2, c, 0]
        for peer in range(1, sections):
            total = total + gath[j % 2, c, peer]
        return [jnp.broadcast_to(total[:, k : k + 1], (per, LANES)) for k in range(count)]

    @pl.when(me == 0)
    def _():
        def clear(s, carry):
            for j in range(ITERS):
                img[j, s] = jnp.zeros((rows, width), jnp.float32)
            return carry

        lax.fori_loop(0, specs, clear, 0)

    @pl.when(me == sections - 1)
    def _():
        def clear(s, carry):
            back[s] = jnp.zeros((rows, width), jnp.float32)
            return carry

        lax.fori_loop(0, per, clear, 0)

    pl.semaphore_wait(barrier, sections - 1)

    state = [{"alpha": [], "beta": []} for _ in range(CHUNKS)]
    for c in range(CHUNKS):
        lead_b[0, c] = jnp.broadcast_to(lead0[c * per : (c + 1) * per, :], (per, LANES))

        def first(s, carry):
            sp = c * per + s
            val = start[sp]
            z[0, sp] = val
            send_scl[0, sp] = coup[sp] * val
            put_shifted(s, val)
            return carry

        lax.fori_loop(0, per, first, 0)
        forward(0, c)

    for c in range(CHUNKS):
        apply(0, c)
        forward(1, c)
    for j in range(ITERS - 1):
        for c in range(CHUNKS):
            st = state[c]
            bias_c = jnp.broadcast_to(bias[c * per : (c + 1) * per, :], (per, LANES))
            sums = totals(j, c, 4 if j == 0 else 3)
            lead_now = lead_b[j, c]
            image_lead = bias_c * lead_now + 0.5 * sums[0]
            if j == 0:
                factor = 1.0 / jnp.sqrt(lead_now * lead_now + sums[3])
                st["factor"] = factor
                alpha = factor * factor * (lead_now * image_lead + sums[1])
                lead_now = lead_now * factor
                image_lead = image_lead * factor
                power = factor * factor * sums[2]
                rest_lead = image_lead - alpha * lead_now
                beta = jnp.sqrt(image_lead * image_lead + power - alpha * alpha + 1e-06)
                inv = factor / beta
                lead_b[0, c] = lead_now
                coef[1] = inv
                coef[2] = -alpha * inv
            else:
                beta_old = st["beta"][-1]
                lead_old = lead_b[j - 1, c]
                alpha = lead_now * image_lead + sums[1]
                rest_lead = image_lead - alpha * lead_now - beta_old * lead_old
                beta = jnp.sqrt(image_lead * image_lead + sums[2] - alpha * alpha - beta_old * beta_old + 1e-06)
                inv = 1.0 / beta
                coef[1] = inv
                coef[2] = -alpha * inv
                coef[3] = -beta_old * inv * (st["factor"] if j == 1 else 1.0)
            lead_b[j + 1, c] = rest_lead / beta
            st["alpha"].append(alpha)
            st["beta"].append(beta)

            def advance(s, carry):
                sp = c * per + s
                val = w_buf[sp] * wide_row(1, s) + z[j, sp] * wide_row(2, s)
                if j > 0:
                    val = val + z[j - 1, sp] * wide_row(3, s)
                z[j + 1, sp] = val
                return carry

            lax.fori_loop(0, per, advance, 0)
            apply(j + 1, c)
            if j + 1 < ITERS - 1:
                forward(j + 2, c)

    lane = lax.broadcasted_iota(jnp.int32, (per, LANES), 1)
    last = ITERS - 1
    for c in range(CHUNKS):
        st = state[c]
        bias_c = jnp.broadcast_to(bias[c * per : (c + 1) * per, :], (per, LANES))
        sums = totals(last, c, 2)
        lead_now = lead_b[last, c]
        alpha = lead_now * (bias_c * lead_now + 0.5 * sums[0]) + sums[1]
        alphas = st["alpha"] + [alpha]
        betas = st["beta"]
        n = ITERS
        zero = jnp.zeros((per, LANES), jnp.float32)
        tri = [[zero] * n for _ in range(n)]
        norm = zero
        for i in range(n):
            tri[i][i] = alphas[i]
            norm = norm + alphas[i] * alphas[i]
            if i + 1 < n:
                tri[i][i + 1] = betas[i]
                tri[i + 1][i] = betas[i]
                norm = norm + 2.0 * (betas[i] * betas[i])
        scale = 0.5 / jnp.sqrt(norm)
        sx = [[tri[i][k] * scale for k in range(n)] for i in range(n)]
        expo = [[zero + (1.0 if i == k else 0.0) for k in range(n)] for i in range(n)]
        for degree in range(12, 0, -1):
            nxt = []
            for i in range(n):
                line = []
                for k in range(n):
                    acc = None
                    for m in range(max(0, i - 1), min(n, i + 2)):
                        term = sx[i][m] * expo[m][k]
                        acc = term if acc is None else acc + term
                    acc = acc * (1.0 / degree)
                    line.append(acc + 1.0 if i == k else acc)
                nxt.append(line)
            expo = nxt
        for _ in range(4):
            nxt = [[None] * n for _ in range(n)]
            for i in range(n):
                for k in range(n):
                    acc = expo[i][0] * expo[0][k]
                    for m in range(1, n):
                        acc = acc + expo[i][m] * expo[m][k]
                    nxt[i][k] = acc
            expo = nxt
        trace = expo[0][0] + expo[1][1] + expo[2][2] + expo[3][3]
        inv = 1.0 / trace
        wt = [[expo[i][k] * inv for k in range(n)] for i in range(n)]
        soft = zero
        gbias = zero
        leads = [lead_b[i, c] for i in range(n)]
        for i in range(n):
            for k in range(n):
                if abs(i - k) <= 1:
                    soft = soft + wt[i][k] * tri[i][k]
                gbias = gbias + wt[i][k] * (leads[i] * leads[k])
        small[c * per : (c + 1) * per, :] = jnp.where(lane == 0, gbias, soft)
        fac = [st["factor"], None, None, None]

        def scaled_by(val, *which):
            for i in which:
                if fac[i] is not None:
                    val = val * fac[i]
            return val

        slot = 0
        pair_slot = {}
        for i in range(n):
            for k in range(i, n):
                val = wt[i][k] if i == k else wt[i][k] + wt[k][i]
                coef[slot] = unit_count * scaled_by(val, i, k)
                pair_slot[i, k] = slot
                slot += 1
        mix_slot = {}
        for i in range(n):
            for k in range(n):
                coef[slot] = -unit_count * scaled_by(wt[i][k], i, k)
                mix_slot[i, k] = slot
                slot += 1
        lin_slot = {}
        for k in range(n):
            val = wt[0][k] * leads[0]
            for i in range(1, n):
                val = val + wt[i][k] * leads[i]
            coef[slot] = math.sqrt(unit_count) * scaled_by(val, k)
            lin_slot[k] = slot
            slot += 1

        def final(s, carry):
            sp = c * per + s
            cf = [coef[k, pl.ds(s, 1), :] for k in range(slot)]
            for g in range(num_groups):
                cols = slice(g * LANES, (g + 1) * LANES)
                zs = [z[i, sp, :, cols] for i in range(n)]
                ims = [img[i, sp, :, cols] for i in range(n)]
                gd = gc = gl = None
                for i in range(n):
                    mixed = zs[i] * cf[pair_slot[i, i]]
                    for k in range(i + 1, n):
                        mixed = mixed + zs[k] * cf[pair_slot[i, k]]
                    mixed_img = ims[0] * cf[mix_slot[i, 0]]
                    for k in range(1, n):
                        mixed_img = mixed_img + ims[k] * cf[mix_slot[i, k]]
                    gd = zs[i] * mixed if gd is None else gd + zs[i] * mixed
                    gc = zs[i] * mixed_img if gc is None else gc + zs[i] * mixed_img
                    lin = zs[i] * cf[lin_slot[i]]
                    gl = lin if gl is None else gl + lin
                grad_diag[sp, :, cols] = gd
                grad_coup[sp, :, cols] = gc
                grad_lin[sp, :, cols] = gl
            return carry

        lax.fori_loop(0, per, final, 0)

    for j in range(ITERS):
        for c in range(CHUNKS):
            each_copy(j, c, True, 0, lambda copy: copy.wait_send())
            if j < ITERS - 1:
                each_copy(j, c, False, 0, lambda copy: copy.wait_send())
            if relayed:
                for images, via in ((True, img_via), (False, scl_via)):
                    if images or j < ITERS - 1:

                        @pl.when(me == via)
                        def _():
                            relay_out(j, c, images).wait_send()


def body(start_lead, start_field, diag_dual, coupling_dual, linear_table, labels, bias_dual, kernels):
    sections = lax.axis_size("layer")
    specs, _, rows, width = start_field.shape
    unit_count = sections * rows * width
    per = specs // CHUNKS
    chan = kernels.shape[-1]
    shape3 = (specs, rows, width)
    full = pl.BlockSpec(memory_space=pltpu.VMEM)
    f32, bf16 = jnp.float32, jnp.bfloat16
    dma = pltpu.SemaphoreType.DMA
    outs = pl.pallas_call(
        functools.partial(kernel_body, sections, float(unit_count)),
        out_shape=[jax.ShapeDtypeStruct(shape3, f32)] * 3 + [jax.ShapeDtypeStruct((specs, LANES), f32)],
        in_specs=[pl.BlockSpec(memory_space=pltpu.SMEM)] + [full] * 7,
        out_specs=[full] * 4,
        scratch_shapes=[
            pltpu.VMEM((ITERS,) + shape3, f32),
            pltpu.VMEM((ITERS,) + shape3, f32),
            pltpu.VMEM((ITERS - 1,) + shape3, f32),
            pltpu.VMEM((ITERS,) + shape3, f32),
            pltpu.VMEM((ITERS - 1,) + shape3, f32),
            pltpu.VMEM(shape3, f32),
            pltpu.VMEM((per, rows, width), f32),
            pltpu.VMEM((per * rows, width + LANES), bf16),
            pltpu.VMEM((per * rows, width + LANES), bf16),
            pltpu.VMEM((4 * chan, 6 * chan), bf16),
            pltpu.VMEM((4 * chan, 6 * chan), bf16),
            pltpu.VMEM((4 * chan, 6 * chan), bf16),
            pltpu.VMEM((4 * chan, 6 * chan), bf16),
            pltpu.VMEM((4, per, LANES), f32),
            pltpu.VMEM((32, per, LANES), f32),
            pltpu.VMEM((ITERS, CHUNKS, per, LANES), f32),
            pltpu.VMEM((2, CHUNKS, per, LANES), f32),
            pltpu.VMEM((2, CHUNKS, sections, per, LANES), f32),
            dma((ITERS, CHUNKS)),
            dma((ITERS, CHUNKS)),
            dma((ITERS - 1, CHUNKS)),
            dma((ITERS - 1, CHUNKS)),
            dma((2, CHUNKS, sections)),
            dma((2, CHUNKS, sections)),
            pltpu.VMEM((ITERS, specs // 2, rows, width), f32),
            dma((ITERS, CHUNKS)),
            dma((ITERS, CHUNKS)),
            dma((ITERS, CHUNKS)),
            dma((ITERS, CHUNKS)),
        ],
        compiler_params=pltpu.CompilerParams(collective_id=0, has_side_effects=True, vmem_limit_bytes=56 * 1024 * 1024),
    )(
        labels,
        start_lead[:, None],
        start_field.reshape(shape3),
        diag_dual.reshape(shape3),
        coupling_dual.reshape(shape3),
        linear_table.reshape(linear_table.shape[0], rows, width),
        bias_dual[:, None],
        kernels.reshape(kernels.shape[1:]),
    )
    big = [out.reshape(start_field.shape) for out in outs[:3]]
    return (*big, outs[3][:, 0], outs[3][:, 1])


def solution(mesh):
    placed = (
        P("spec"),
        P("spec", "layer", None, None),
        P("spec", "layer", None, None),
        P("spec", "layer", None, None),
        P(None, "layer", None, None),
        P("spec"),
        P("spec"),
        P("layer", None, None, None, None),
    )
    return jax.shard_map(
        body,
        mesh=mesh,
        in_specs=placed,
        out_specs=(
            P("spec", "layer", None, None),
            P("spec", "layer", None, None),
            P("spec", "layer", None, None),
            P("spec"),
            P("spec"),
        ),
        check_vma=False,
    )
```
